32 devices in a mesh: crop: 1, res: 32 (over z, y, x, core).
Axes of the slice: x: 2, y: 2, z: 4, core: 2. Of those that a mesh axis runs over, the one named last changes fastest.
Arguments:
- homolog_symbol_ids: int32 [64, 128], P(('crop', 'res')), may hold values from 0 to 22
- residue_attend_mask: int32 [128], P('crop'), may hold values 0 or 1
- alignment_state: bfloat16 [64, 128, 256], P(('crop', 'res')), may hold values from -6 to 6
- pair: bfloat16 [128, 128, 128], P(('crop', 'res')), may hold values from -6 to 6
- symbol_lookup_matrix: bfloat16 [23, 256], replicated, may hold values from -3 to 3
- pair_bias_weight: bfloat16 [128, 8], replicated, may hold values from -0.5 to 0.5
- row_projection_weight: bfloat16 [256, 1024], replicated, may hold values from -8 to 8
- horizontal_readout_matrix: bfloat16 [256, 256], replicated, may hold values from -0.375 to 0.375
- column_projection_weight: bfloat16 [256, 1024], replicated, may hold values from -8 to 8
- vertical_readout_matrix: bfloat16 [256, 256], replicated, may hold values from -0.375 to 0.375
- product_factor_matrices: bfloat16 [256, 64], replicated, may hold values from -0.375 to 0.375
- outer_output_weight: bfloat16 [1024, 128], replicated, may hold values from -1.5 to 1.5
- triangle_input_weight: bfloat16 [128, 640], replicated, may hold values from -0.5 to 0.5
- triangle_output_weight: bfloat16 [128, 128], replicated, may hold values from -0.5 to 0.5
Outputs:
- alignment_output: bfloat16 [64, 128, 256], P('crop', 'res')
- pair_output: bfloat16 [128, 128, 128], P(('crop', 'res'))
The draws below stay inside these ranges and needn't reach their ends.
All inputs are finite; a program needn't handle non-finite values.
Results may differ from the reference program's by a relative error of at most 0.013.
Values may be sent and summed in bfloat16 or wider, within the bound.
A program may use at most 64 MiB of HBM per device.

```python
import jax
import jax.numpy as jnp
from jax import lax

FEATURE_DEPTH = 256
CZ = 128
HEAD_NUMBER = 8
PRODUCT_WIDTH = 32
AMINO_VOCAB = 23
HOMOLOG_NUMBER = 64
CHAIN_LENGTH = 128


def draw_alignment_state(key, part):
    random_seed_primary = jax.random.fold_in(jax.random.fold_in(key, 3), 0)
    lower_bound_index = jax.random.normal(random_seed_primary, (HOMOLOG_NUMBER, CHAIN_LENGTH, FEATURE_DEPTH), jnp.float32)
    return jnp.clip(lower_bound_index, -6.0, 6.0).astype(jnp.bfloat16)


def draw_projection(key, channels):
    weight = jnp.clip(jax.random.normal(key, (channels, 4 * channels), jnp.float32), -4.0, 4.0) * channels ** (-0.5)
    return weight.astype(jnp.bfloat16)


def draw_row_projection_weight(key, part):
    return draw_projection(jax.random.fold_in(key, 11), FEATURE_DEPTH)


def draw_column_projection_weight(key, part):
    return draw_projection(jax.random.fold_in(key, 29), FEATURE_DEPTH)


def touch_ends(result, key, smallest, high):
    extent = result.shape
    place = [jax.random.randint(jax.random.fold_in(key, axis), (), 0, extent[axis]) for axis in range(len(extent))]
    result = result.at[tuple(place)].set(smallest)
    longest = extent.index(max(extent))
    place[longest] = (place[longest] + 1) % extent[longest]
    return result.at[tuple(place)].set(high)


def shard_levels(key, shape, pieces, smallest, largest):
    factor_of, own = 1.0, jax.random.fold_in(key, 6)
    for position, blocks in pieces:
        heights = jnp.exp(jax.random.uniform(jax.random.fold_in(own, position), (blocks,), jnp.float32, smallest / len(pieces), largest / len(pieces)))
        factor_of = factor_of * jnp.repeat(heights, shape[position] // blocks).reshape([-1 if axis == position else 1 for axis in range(len(shape))])
    return factor_of


def bell_draw(key, extent, scale, reach, cuts=(), kind=jnp.bfloat16):
    loudness = shard_levels(key, extent, cuts, -0.22, 0.18) if cuts else 1.0
    entries = jax.random.normal(key, extent, jnp.float32) * scale * loudness
    return jnp.minimum(jnp.maximum(entries, -reach), reach).astype(kind)


def setup_inputs(seed: int = 0, part: int = 0) -> dict:
    seeds = jax.random.split(jax.random.key(seed), 15)
    part_keys = jax.random.split(jax.random.fold_in(seeds[14], part), 15)
    homolog_symbol_ids = touch_ends(jax.random.randint(part_keys[0], (HOMOLOG_NUMBER, CHAIN_LENGTH), 0, AMINO_VOCAB), jax.random.fold_in(part_keys[0], 1), 0, AMINO_VOCAB - 1).astype(jnp.int32)
    residue_attend_mask = touch_ends((jax.random.randint(part_keys[1], (CHAIN_LENGTH,), 0, 8) < 7).astype(jnp.int32), jax.random.fold_in(part_keys[1], 1), 0, 1)
    alignment_state = draw_alignment_state(jax.random.fold_in(jax.random.fold_in(seeds[14], part), 71), part)
    pair = bell_draw(part_keys[3], (CHAIN_LENGTH, CHAIN_LENGTH, CZ), 1.0, 6.0, ((0, 32),))
    symbol_lookup_matrix = bell_draw(seeds[4], (AMINO_VOCAB, FEATURE_DEPTH), 0.5, 3.0)
    pair_bias_weight = bell_draw(seeds[5], (CZ, HEAD_NUMBER), CZ ** -0.5, 0.5)
    row_projection_weight = draw_row_projection_weight(jax.random.fold_in(seeds[14], 71), part)
    horizontal_readout_matrix = bell_draw(seeds[7], (FEATURE_DEPTH, FEATURE_DEPTH), FEATURE_DEPTH ** -0.5, 0.375)
    column_projection_weight = draw_column_projection_weight(jax.random.fold_in(seeds[14], 71), part)
    vertical_readout_matrix = bell_draw(seeds[9], (FEATURE_DEPTH, FEATURE_DEPTH), FEATURE_DEPTH ** -0.5, 0.375)
    product_factor_matrices = bell_draw(seeds[10], (FEATURE_DEPTH, 2 * PRODUCT_WIDTH), FEATURE_DEPTH ** -0.5, 0.375)
    outer_output_weight = bell_draw(seeds[11], (PRODUCT_WIDTH * PRODUCT_WIDTH, CZ), (PRODUCT_WIDTH * PRODUCT_WIDTH // 64) ** -0.5, 1.5)
    triangle_input_weight = bell_draw(seeds[12], (CZ, 5 * CZ), CZ ** -0.5, 0.5)
    triangle_output_weight = bell_draw(seeds[13], (CZ, CZ), CZ ** -0.5, 0.5)
    return dict(homolog_symbol_ids=homolog_symbol_ids, residue_attend_mask=residue_attend_mask, alignment_state=alignment_state, pair=pair, symbol_lookup_matrix=symbol_lookup_matrix, pair_bias_weight=pair_bias_weight, row_projection_weight=row_projection_weight, horizontal_readout_matrix=horizontal_readout_matrix, column_projection_weight=column_projection_weight, vertical_readout_matrix=vertical_readout_matrix, product_factor_matrices=product_factor_matrices, outer_output_weight=outer_output_weight, triangle_input_weight=triangle_input_weight, triangle_output_weight=triangle_output_weight)


EPSILON = 1e-05

def layer_normalized(input_rows, axis):
    average = lax.optimization_barrier(jnp.mean(input_rows, axis, keepdims=True))
    centred = input_rows - average
    spread = lax.optimization_barrier(jnp.mean(centred * centred, axis, keepdims=True))
    return centred * lax.rsqrt(spread + EPSILON)

def split_proj(input_rows, weight):
    channels = weight.shape[0]
    head_size = channels // HEAD_NUMBER
    projected = jnp.dot(input_rows, weight, preferred_element_type=jnp.float32)
    query_tensor = (projected[:, :channels] * head_size ** (-0.5)).astype(jnp.bfloat16).reshape(-1, HEAD_NUMBER, head_size)
    key_tensor = projected[:, channels:2 * channels].astype(jnp.bfloat16).reshape(-1, HEAD_NUMBER, head_size)
    value_tensor = projected[:, 2 * channels:3 * channels].astype(jnp.bfloat16).reshape(-1, HEAD_NUMBER, head_size)
    gate_values = projected[:, 3 * channels:]
    return (query_tensor, key_tensor, value_tensor, gate_values)

def gated_attention(query_tensor, key_tensor, value_tensor, gate_values, extra_bias, out_weight):
    scores = jnp.einsum('qhd,khd->hqk', query_tensor.astype(jnp.float32), key_tensor.astype(jnp.float32)) + extra_bias
    row_top = lax.optimization_barrier(jnp.max(scores, -1, keepdims=True))
    exp_scores = jnp.exp(scores - row_top)
    weights = (exp_scores / lax.optimization_barrier(jnp.sum(exp_scores, -1, keepdims=True))).astype(jnp.bfloat16)
    mixed = jnp.einsum('hqk,khd->qhd', weights.astype(jnp.float32), value_tensor.astype(jnp.float32))
    gated = (jax.nn.sigmoid(gate_values) * mixed.reshape(gate_values.shape)).astype(jnp.bfloat16)
    return jnp.dot(gated, out_weight, preferred_element_type=jnp.float32)

def reference(homolog_symbol_ids, residue_attend_mask, alignment_state, pair, symbol_lookup_matrix, pair_bias_weight, row_projection_weight, horizontal_readout_matrix, column_projection_weight, vertical_readout_matrix, product_factor_matrices, outer_output_weight, triangle_input_weight, triangle_output_weight):
    one_hot_tokens = (homolog_symbol_ids[:, :, None] == jnp.arange(AMINO_VOCAB, dtype=jnp.int32)[None, None, :]).astype(jnp.float32)
    alignment_initial = alignment_state.astype(jnp.float32) + jnp.einsum('kly,yb->klb', one_hot_tokens, symbol_lookup_matrix.astype(jnp.float32))
    pair_normed = layer_normalized(pair.astype(jnp.float32), -1).astype(jnp.bfloat16)
    bias_full = jnp.einsum('ijc,ch->hij', pair_normed.astype(jnp.float32), pair_bias_weight.astype(jnp.float32)).astype(jnp.bfloat16)
    mask_bias = (residue_attend_mask.astype(jnp.float32) - 1.0) * 10000.0
    extra_bias = bias_full.astype(jnp.float32) + mask_bias[None, None, :]

    def row_update_one(alignment_row):
        input_rows = layer_normalized(alignment_row, -1).astype(jnp.bfloat16)
        query_tensor, key_tensor, value_tensor, gate_values = split_proj(input_rows, row_projection_weight)
        return (alignment_row + gated_attention(query_tensor, key_tensor, value_tensor, gate_values, extra_bias, horizontal_readout_matrix)).astype(jnp.bfloat16)
    alignment_after_rows = lax.map(row_update_one, alignment_initial)

    def column_update_one(column):
        column_start = column.astype(jnp.float32)
        input_rows = layer_normalized(column_start, -1).astype(jnp.bfloat16)
        query_tensor, key_tensor, value_tensor, gate_values = split_proj(input_rows, column_projection_weight)
        return column_start + gated_attention(query_tensor, key_tensor, value_tensor, gate_values, jnp.float32(0.0), vertical_readout_matrix)
    alignment_after_columns = lax.map(column_update_one, jnp.swapaxes(alignment_after_rows, 0, 1))
    alignment_output = jnp.swapaxes(alignment_after_columns, 0, 1).astype(jnp.bfloat16)
    outer_input = layer_normalized(alignment_after_columns, -1).astype(jnp.bfloat16)
    factor_ab = jnp.einsum('rsc,ce->rse', outer_input.astype(jnp.float32), product_factor_matrices.astype(jnp.float32))
    left = factor_ab[..., :PRODUCT_WIDTH].astype(jnp.bfloat16)
    latter_factor = factor_ab[..., PRODUCT_WIDTH:].astype(jnp.bfloat16)

    def opm_one(former_factor_vector):
        cross_product_result = (jnp.einsum('vf,avt->aft', former_factor_vector.astype(jnp.float32), latter_factor.astype(jnp.float32)) / HOMOLOG_NUMBER).astype(jnp.bfloat16)
        return jnp.dot(cross_product_result.reshape(CHAIN_LENGTH, PRODUCT_WIDTH * PRODUCT_WIDTH), outer_output_weight, preferred_element_type=jnp.float32)
    update = lax.map(opm_one, left)
    pair_one = pair.astype(jnp.float32) + update
    tri_normed = layer_normalized(pair_one, -1).astype(jnp.bfloat16)
    projected = jnp.einsum('ijc,ce->ije', tri_normed.astype(jnp.float32), triangle_input_weight.astype(jnp.float32))
    left_f = (jax.nn.sigmoid(projected[..., CZ:2 * CZ]) * projected[..., :CZ]).astype(jnp.bfloat16)
    right_f = (jax.nn.sigmoid(projected[..., 3 * CZ:4 * CZ]) * projected[..., 2 * CZ:3 * CZ]).astype(jnp.bfloat16)
    gate_out = projected[..., 4 * CZ:]
    combined = jnp.einsum('ikc,jkc->ijc', left_f.astype(jnp.float32), right_f.astype(jnp.float32)).astype(jnp.bfloat16)
    comb_normed = layer_normalized(combined.astype(jnp.float32), -1).astype(jnp.bfloat16)
    tri_update = jnp.dot(comb_normed, triangle_output_weight, preferred_element_type=jnp.float32)
    pair_output = (pair_one + jax.nn.sigmoid(gate_out) * tri_update).astype(jnp.bfloat16)
    return (alignment_output, pair_output)
```

```python
import functools

import jax
import jax.numpy as jnp
from jax import lax
from jax.experimental import pallas as pl
from jax.experimental.pallas import tpu as pltpu
from jax.sharding import PartitionSpec as P

EPSILON = 1e-05
MESH = pl.DeviceIdType.MESH


def exchange_kernel(count, gather, source, landing, send_sem, recv_sem):
    me = lax.axis_index("res")
    barrier = pltpu.get_barrier_semaphore()

    @pl.loop(1, count)
    def _(step):
        pl.semaphore_signal(
            barrier,
            inc=1,
            device_id={"res": lax.rem(me + step, count)},
            device_id_type=MESH,
        )

    landing[me] = source[...] if gather else source[me]
    pl.semaphore_wait(barrier, count - 1)

    @pl.loop(1, count)
    def _(step):
        peer = lax.rem(me + step, count)
        pltpu.make_async_remote_copy(
            src_ref=source if gather else source.at[peer],
            dst_ref=landing.at[me],
            send_sem=send_sem,
            recv_sem=recv_sem,
            device_id={"res": peer},
            device_id_type=MESH,
        ).start()

    others = landing.at[pl.ds(0, count - 1)]
    pltpu.make_async_copy(others, others, recv_sem).wait()
    pltpu.make_async_copy(others, others, send_sem).wait()


def exchange(operand, gather, number):
    count = lax.axis_size("res")
    extent = operand.shape if gather else operand.shape[1:]
    return pl.pallas_call(
        functools.partial(exchange_kernel, count, gather),
        out_shape=jax.ShapeDtypeStruct((count,) + extent, operand.dtype),
        in_specs=[pl.BlockSpec(memory_space=pltpu.VMEM)],
        out_specs=pl.BlockSpec(memory_space=pltpu.VMEM),
        scratch_shapes=[pltpu.SemaphoreType.DMA, pltpu.SemaphoreType.DMA],
        compiler_params=pltpu.CompilerParams(
            collective_id=number, has_side_effects=True
        ),
    )(operand)


def layer_normalized(input_rows, axis):
    average = jnp.mean(input_rows, axis, keepdims=True)
    centred = input_rows - average
    spread = jnp.mean(centred * centred, axis, keepdims=True)
    return centred * lax.rsqrt(spread + EPSILON)


def split_proj(input_rows, weight, head_count):
    channels = weight.shape[0]
    head_size = channels // head_count
    projected = jnp.einsum("blc,ce->ble", input_rows, weight, preferred_element_type=jnp.float32)
    lead = projected.shape[:2]
    query_tensor = (
        (projected[..., :channels] * head_size ** (-0.5))
        .astype(jnp.bfloat16)
        .reshape(lead + (head_count, head_size))
    )
    key_tensor = (
        projected[..., channels : 2 * channels]
        .astype(jnp.bfloat16)
        .reshape(lead + (head_count, head_size))
    )
    value_tensor = (
        projected[..., 2 * channels : 3 * channels]
        .astype(jnp.bfloat16)
        .reshape(lead + (head_count, head_size))
    )
    gate_values = projected[..., 3 * channels :]
    return (query_tensor, key_tensor, value_tensor, gate_values)


def attention_block_fn(query_tensor, key_tensor, value_tensor, gate_values, extra_bias, out_weight):
    scores = (
        jnp.einsum("bqhd,bkhd->bhqk", query_tensor, key_tensor, preferred_element_type=jnp.float32)
        + extra_bias
    )
    row_top = jnp.max(scores, -1, keepdims=True)
    exp_scores = jnp.exp(scores - row_top)
    weights = (exp_scores / jnp.sum(exp_scores, -1, keepdims=True)).astype(jnp.bfloat16)
    mixed = jnp.einsum("bhqk,bkhd->bqhd", weights, value_tensor, preferred_element_type=jnp.float32)
    gated = (jax.nn.sigmoid(gate_values) * mixed.reshape(gate_values.shape)).astype(jnp.bfloat16)
    return jnp.einsum("bqc,ce->bqe", gated, out_weight, preferred_element_type=jnp.float32)


def shards(
    homolog_symbol_ids,
    residue_attend_mask,
    alignment_state,
    pair,
    symbol_lookup_matrix,
    pair_bias_weight,
    row_projection_weight,
    horizontal_readout_matrix,
    column_projection_weight,
    vertical_readout_matrix,
    product_factor_matrices,
    outer_output_weight,
    triangle_input_weight,
    triangle_output_weight,
):
    residue_count = lax.axis_size("res")
    sequence_total = alignment_state.shape[0] * residue_count
    res_local = pair.shape[0]
    chain_total = pair.shape[1]
    pair_chan = pair.shape[2]
    owner_chan = pair_chan // residue_count
    outer_chan = product_factor_matrices.shape[1] // 2
    head_count = pair_bias_weight.shape[1]
    token_class_count = symbol_lookup_matrix.shape[0]
    one_hot_tokens = (
        homolog_symbol_ids[:, :, None]
        == jnp.arange(token_class_count, dtype=jnp.int32)[None, None, :]
    ).astype(jnp.bfloat16)
    alignment_initial = alignment_state.astype(jnp.float32) + jnp.einsum(
        "kly,yb->klb", one_hot_tokens, symbol_lookup_matrix, preferred_element_type=jnp.float32
    )
    pair_normed = layer_normalized(pair.astype(jnp.float32), -1).astype(jnp.bfloat16)
    bias_local = jnp.einsum(
        "ijc,ch->hij", pair_normed, pair_bias_weight, preferred_element_type=jnp.float32
    ).astype(jnp.bfloat16)
    mask_bias = (residue_attend_mask.astype(jnp.float32) - 1.0) * 10000.0
    row_input = layer_normalized(alignment_initial, -1).astype(jnp.bfloat16)
    query_tensor, key_tensor, value_tensor, gate_values = split_proj(
        row_input, row_projection_weight, head_count
    )
    bias_all = exchange(bias_local.reshape(-1, chain_total), True, 0)
    bias_all = jnp.swapaxes(
        bias_all.reshape(residue_count, head_count, res_local, chain_total), 0, 1
    ).reshape(head_count, chain_total, chain_total)
    extra_bias = bias_all.astype(jnp.float32)[None] + mask_bias[None, None, None, :]
    row_attention_update = attention_block_fn(
        query_tensor, key_tensor, value_tensor, gate_values, extra_bias, horizontal_readout_matrix
    )
    alignment_after_rows = (alignment_initial + row_attention_update).astype(jnp.bfloat16)
    seqs_local, channels = alignment_state.shape[0], alignment_state.shape[2]
    outgoing = jnp.swapaxes(
        alignment_after_rows.reshape(seqs_local, residue_count, res_local, channels), 0, 1
    )
    alignment_columns = exchange(
        outgoing.reshape(residue_count, -1, 2 * channels), False, 1
    ).reshape(sequence_total, res_local, channels)
    column_start = jnp.swapaxes(alignment_columns, 0, 1).astype(jnp.float32)
    col_in = layer_normalized(column_start, -1).astype(jnp.bfloat16)
    col_queries, col_keys, col_values, col_gating = split_proj(
        col_in, column_projection_weight, head_count
    )
    alignment_after_columns = column_start + attention_block_fn(
        col_queries, col_keys, col_values, col_gating, jnp.float32(0.0), vertical_readout_matrix
    )
    alignment_output = jnp.swapaxes(alignment_after_columns, 0, 1).astype(jnp.bfloat16)
    outer_input = layer_normalized(alignment_after_columns, -1).astype(jnp.bfloat16)
    factor_ab = jnp.einsum(
        "rsc,ce->rse", outer_input, product_factor_matrices, preferred_element_type=jnp.float32
    )
    left = factor_ab[..., :outer_chan].astype(jnp.bfloat16)
    latter_factor = (
        factor_ab[..., outer_chan:]
        .astype(jnp.bfloat16)
        .reshape(res_local, sequence_total * outer_chan)
    )
    piece = exchange(latter_factor.reshape(-1, 128), True, 2)
    count = chain_total
    right_rows = piece.reshape(count, sequence_total, outer_chan)
    cross_product_result = (
        jnp.einsum("isc,jsd->ijcd", left, right_rows, preferred_element_type=jnp.float32)
        / sequence_total
    ).astype(jnp.bfloat16)
    update = jnp.einsum(
        "ije,ez->ijz",
        cross_product_result.reshape(res_local, count, outer_chan * outer_chan),
        outer_output_weight,
        preferred_element_type=jnp.float32,
    )
    pair_one = pair.astype(jnp.float32) + update
    tri_normed = layer_normalized(pair_one, -1).astype(jnp.bfloat16)
    factors = jnp.einsum(
        "ijc,ce->eij",
        tri_normed,
        triangle_input_weight[:, : 4 * pair_chan],
        preferred_element_type=jnp.float32,
    )
    gate_out = jnp.einsum(
        "ijc,ce->ije",
        tri_normed,
        triangle_input_weight[:, 4 * pair_chan :],
        preferred_element_type=jnp.float32,
    )
    left_f = (jax.nn.sigmoid(factors[pair_chan : 2 * pair_chan]) * factors[:pair_chan]).astype(
        jnp.bfloat16
    )
    right_f = (
        jax.nn.sigmoid(factors[3 * pair_chan :]) * factors[2 * pair_chan : 3 * pair_chan]
    ).astype(jnp.bfloat16)
    left_f = left_f.reshape(residue_count, owner_chan, res_local, chain_total)
    right_f = right_f.reshape(residue_count, owner_chan, res_local, chain_total)
    both = jnp.concatenate([left_f, right_f], axis=1)
    both = exchange(both.reshape(residue_count, -1, chain_total), False, 3)
    both = both.reshape(residue_count, 2, owner_chan, res_local, chain_total)
    both = jnp.transpose(both, (1, 2, 0, 3, 4)).reshape(
        2, owner_chan, chain_total, chain_total
    )
    combined = jnp.einsum(
        "cik,cjk->cij", both[0], both[1], preferred_element_type=jnp.float32
    ).astype(jnp.bfloat16)
    combined = jnp.swapaxes(
        combined.reshape(owner_chan, residue_count, res_local, chain_total), 0, 1
    )
    back_rows = exchange(combined.reshape(residue_count, -1, chain_total), False, 4)
    back_rows = back_rows.reshape(pair_chan, res_local, chain_total)
    comb_normed = layer_normalized(back_rows.astype(jnp.float32), 0).astype(jnp.bfloat16)
    tri_update = jnp.einsum(
        "cij,cz->ijz", comb_normed, triangle_output_weight, preferred_element_type=jnp.float32
    )
    pair_output = (pair_one + jax.nn.sigmoid(gate_out) * tri_update).astype(jnp.bfloat16)
    return (alignment_output, pair_output)


def solution(mesh):
    placed = (
        P(("crop", "res"), None),
        P("crop"),
        P(("crop", "res"), None, None),
        P(("crop", "res"), None, None),
        P(),
        P(),
        P(),
        P(),
        P(),
        P(),
        P(),
        P(),
        P(),
        P(),
    )
    return jax.shard_map(
        shards,
        mesh=mesh,
        in_specs=placed,
        out_specs=(P("crop", "res", None), P(("crop", "res"), None, None)),
        check_vma=False,
    )
```

```python
import functools

import jax
import jax.numpy as jnp
from jax import lax
from jax.experimental import pallas as pl
from jax.experimental.pallas import tpu as pltpu
from jax.sharding import PartitionSpec as P

EPSILON = 1e-05
MESH = pl.DeviceIdType.MESH
F32 = jnp.float32
BF16 = jnp.bfloat16
LANES = 128
SUBLANES = 8


def normalized(rows, axis=-1):
    average = jnp.mean(rows, axis, keepdims=True)
    centred = rows - average
    spread = jnp.mean(centred * centred, axis, keepdims=True)
    return (centred * lax.rsqrt(spread + EPSILON)).astype(BF16)


def product(lhs, rhs, lhs_axis=1, rhs_axis=0):
    return lax.dot_general(
        lhs, rhs, (((lhs_axis,), (rhs_axis,)), ((), ())), preferred_element_type=F32
    )


def permutation(size, major, minor):
    shift = minor.bit_length() - 1
    out = lax.broadcasted_iota(jnp.int32, (size, size), 0)
    came = lax.broadcasted_iota(jnp.int32, (size, size), 1)
    wanted = (out & (minor - 1)) * major + (out >> shift)
    return jnp.where(wanted == came, 1.0, 0.0).astype(BF16)


def swap_halves(first, second):
    half = SUBLANES // 2
    shape = first.shape
    first = first.reshape(-1, SUBLANES, shape[-1])
    second = second.reshape(-1, SUBLANES, shape[-1])
    upper = lax.broadcasted_iota(jnp.int32, first.shape, 1) < half
    low = jnp.where(upper, first, pltpu.roll(second, half, 1))
    high = jnp.where(upper, pltpu.roll(first, half, 1), second)
    return low.reshape(shape), high.reshape(shape)


def strided(wide, first, rows, stride):
    return jnp.concatenate(
        [wide[t, pl.ds(first, rows, stride=stride), :] for t in range(wide.shape[0])], 1
    )


def spread_tiles(wide, rows):
    for t in range(wide.shape[0]):
        wide[t] = rows[:, t * LANES : (t + 1) * LANES]


def attention(projected, channels, head_size, extra):
    rows = projected.shape[0]
    per_tile = LANES // head_size
    owner = lax.broadcasted_iota(jnp.int32, (rows, LANES), 1) >> (head_size.bit_length() - 1)
    pieces = []
    for tile in range(channels // LANES):
        part = lambda block: projected[:, block * channels + tile * LANES :][:, :LANES]
        query = part(0) * head_size ** (-0.5)
        key = part(1).astype(BF16)
        value = part(2)
        queries = jnp.concatenate(
            [jnp.where(owner == t, query, 0.0).astype(BF16) for t in range(per_tile)], 0
        )
        values = jnp.concatenate(
            [jnp.where(owner == t, value, 0.0).astype(BF16) for t in range(per_tile)], 0
        )
        scores = product(queries, key, 1, 1) + jnp.concatenate(
            [extra(tile * per_tile + t) for t in range(per_tile)], 0
        )
        top = jnp.max(scores, -1, keepdims=True)
        raised = jnp.exp(scores - top)
        weights = (raised * (1.0 / jnp.sum(raised, -1, keepdims=True))).astype(BF16)
        weights = jnp.concatenate(
            [weights[t * rows : (t + 1) * rows] for t in range(per_tile)], 1
        )
        mixed = product(weights, values)
        pieces.append((jax.nn.sigmoid(part(3)) * mixed).astype(BF16))
    return jnp.concatenate(pieces, 1)


def block_kernel(
    count,
    ids,
    mask,
    state,
    pair,
    lookup,
    bias_weight,
    row_weight,
    row_readout,
    column_weight,
    column_readout,
    factor_weight,
    outer_weight,
    tri_weight,
    tri_out_weight,
    msa_out,
    pair_out,
    bias_land,
    bias_wide,
    msa_send,
    msa_land,
    right_land,
    outer_wide,
    folded,
    tri_wide,
    tri_send,
    tri_land,
    back_send,
    back_land,
    back_wide,
    send_sems,
    recv_sems,
):
    me = lax.axis_index("res")
    seqs, chain, channels = state.shape
    owned, _, pair_chan = pair.shape
    heads = bias_weight.shape[1]
    head_size = channels // heads
    total = seqs * count
    classes = lookup.shape[0]
    width = factor_weight.shape[1] // 2
    held = pair_chan // count

    barrier = pltpu.get_barrier_semaphore()

    @pl.loop(1, count)
    def _(step):
        pl.semaphore_signal(
            barrier,
            inc=1,
            device_id={"res": lax.rem(me + step, count)},
            device_id_type=MESH,
        )

    def send(phase, landing, outgoing=None):
        @pl.loop(1, count)
        def _(step):
            peer = lax.rem(me + step, count)
            pltpu.make_async_remote_copy(
                src_ref=landing.at[me] if outgoing is None else outgoing.at[peer],
                dst_ref=landing.at[me],
                send_sem=send_sems.at[phase],
                recv_sem=recv_sems.at[phase],
                device_id={"res": peer},
                device_id_type=MESH,
            ).start()

    def drain(sems, phase, landing):
        others = landing.at[pl.ds(0, count - 1)]
        pltpu.make_async_copy(others, others, sems.at[phase]).wait()

    pair_rows = pair[...].astype(F32).reshape(owned * chain, pair_chan)
    bias = product(bias_weight[...], normalized(pair_rows), 0, 1)
    bias_land[me] = jnp.concatenate(
        [bias[:, i * chain : (i + 1) * chain] for i in range(owned)], 0
    ).astype(BF16)
    pl.semaphore_wait(barrier, count - 1)
    send(0, bias_land)

    starts = []
    for s in range(seqs):
        symbols = lax.broadcasted_iota(jnp.int32, (classes, chain), 0)
        hot = jnp.where(symbols == ids[s : s + 1, :], 1.0, 0.0).astype(BF16)
        starts.append(state[s].astype(F32) + product(hot, lookup[...], 0, 0))
    start = jnp.concatenate(starts, 0)
    projected = product(normalized(start), row_weight[...])
    masked = (mask[...].astype(F32) - 1.0) * 10000.0
    drain(recv_sems, 0, bias_land)
    spread_tiles(bias_wide, bias_land[...].astype(F32).reshape(-1, chain) + masked)
    extra = lambda head: strided(bias_wide, head, chain, heads)
    gated = jnp.concatenate(
        [
            attention(projected[s * chain : (s + 1) * chain], channels, head_size, extra)
            for s in range(seqs)
        ],
        0,
    )
    after_rows = (start + product(gated, row_readout[...])).astype(BF16)

    size = seqs * chain
    out = lax.broadcasted_iota(jnp.int32, (size, size), 0)
    came = lax.broadcasted_iota(jnp.int32, (size, size), 1)
    low_bits, seq_bits = owned.bit_length() - 1, seqs.bit_length() - 1
    wanted = (
        ((out >> low_bits) & (seqs - 1)) * chain
        + (out >> (low_bits + seq_bits)) * owned
        + (out & (owned - 1))
    )
    order = jnp.where(wanted == came, 1.0, 0.0).astype(BF16)
    moved = product(order, after_rows)
    group = seqs * owned
    msa_send[...] = jnp.concatenate(
        [
            moved[:, t * LANES : (t + 1) * LANES].reshape(count, group, LANES)
            for t in range(channels // LANES)
        ],
        1,
    ).astype(BF16)
    msa_land[me] = msa_send[me]
    send(1, msa_land, msa_send)
    outer_wide[...] = outer_weight[...].astype(F32)
    by_residue = permutation(total * owned, owned, total)
    by_sequence = permutation(total * owned, total, owned)
    drain(recv_sems, 1, msa_land)

    arrived = msa_land[...].astype(F32)
    arrived = jnp.concatenate(
        [
            arrived[:, t * group : (t + 1) * group].reshape(total * owned, LANES)
            for t in range(channels // LANES)
        ],
        1,
    ).astype(BF16)
    columns = product(by_residue, arrived)
    projected = product(normalized(columns), column_weight[...])
    joined = max(total, LANES)
    bits = total.bit_length() - 1
    same = (lax.broadcasted_iota(jnp.int32, (joined, joined), 0) >> bits) == (
        lax.broadcasted_iota(jnp.int32, (joined, joined), 1) >> bits
    )
    apart = jnp.where(same, 0.0, -1e30)
    gated = jnp.concatenate(
        [
            attention(projected[g : g + joined], channels, head_size, lambda head: apart)
            for g in range(0, total * owned, joined)
        ],
        0,
    )
    after = columns + product(gated, column_readout[...])

    outer_in = normalized(after)
    left = product(outer_in, factor_weight[...])[:, :width].astype(BF16)
    right = product(factor_weight[...], outer_in, 0, 1)[width:]
    packed = LANES // total
    slots = width // packed
    right = jnp.concatenate(
        [
            jnp.concatenate(
                [
                    right[p * slots : (p + 1) * slots, r * total : (r + 1) * total]
                    for p in range(packed)
                ],
                1,
            )
            for r in range(owned)
        ],
        0,
    ).astype(BF16)
    right_land[me] = product(permutation(slots * owned, slots, owned), right).astype(BF16)
    send(2, right_land)
    msa_out[...] = product(by_sequence, after.astype(BF16)).astype(BF16)
    for k in range(width):
        slot, p = k // packed, k % packed
        weight = outer_wide[pl.ds(p * slots + slot, width, stride=width), :].astype(BF16)
        part = product(left, weight).astype(BF16)
        for i in range(owned):
            folded[k * total : (k + 1) * total, i * pair_chan : (i + 1) * pair_chan] = part[
                i * total : (i + 1) * total
            ]
    drain(recv_sems, 2, right_land)
    wide = right_land[...].astype(F32)
    tiles = slots * owned // SUBLANES
    wide = wide.reshape(count // 2, 2, tiles, SUBLANES, LANES)
    low, high = swap_halves(wide[:, 0], wide[:, 1])
    right_rows = jnp.concatenate(
        [
            half[:, t].reshape(chain, LANES).astype(BF16)
            for t in range(tiles)
            for half in (low, high)
        ],
        1,
    )
    update = product(right_rows, folded[...]) * (1.0 / total)
    pair_one = pair_rows + jnp.concatenate(
        [update[:, i * pair_chan : (i + 1) * pair_chan] for i in range(owned)], 0
    )

    tri_in = normalized(pair_one)
    factors = product(tri_weight[:, : 4 * pair_chan], tri_in, 0, 1)
    for side in range(2):
        plain = factors[2 * side * pair_chan : (2 * side + 1) * pair_chan]
        gate = factors[(2 * side + 1) * pair_chan : (2 * side + 2) * pair_chan]
        factor = jax.nn.sigmoid(gate) * plain
        for i in range(owned):
            for t in range(chain // LANES):
                tri_wide[t, pl.ds(side * owned + i, pair_chan, stride=2 * owned), :] = factor[
                    :, i * chain + t * LANES :
                ][:, :LANES]
    tri_send[...] = (
        jnp.concatenate([tri_wide[t] for t in range(chain // LANES)], 1)
        .astype(BF16)
        .reshape(tri_send.shape)
    )
    tri_land[me] = tri_send[me]
    send(3, tri_land, tri_send)
    gate_out = jax.nn.sigmoid(product(tri_in, tri_weight[:, 4 * pair_chan :]))
    drain(recv_sems, 3, tri_land)
    wide = tri_land[...].astype(F32).reshape(count // 2, 2, held, SUBLANES, chain)
    low, high = swap_halves(wide[:, 0], wide[:, 1])
    combined = [
        product(
            low[:, c].reshape(chain, chain).astype(BF16),
            high[:, c].reshape(chain, chain).astype(BF16),
            1,
            1,
        ).reshape(count // 2, SUBLANES, chain)
        for c in range(held)
    ]
    swapped = [swap_halves(combined[c], combined[c + 1]) for c in range(0, held, 2)]
    even = jnp.concatenate([low for low, _ in swapped], 1)
    odd = jnp.concatenate([high for _, high in swapped], 1)
    back_send[...] = (
        jnp.concatenate([even[:, None], odd[:, None]], 1)
        .reshape(back_send.shape)
        .astype(BF16)
    )
    back_land[me] = back_send[me]
    send(4, back_land, back_send)
    drain(recv_sems, 4, back_land)
    spread_tiles(back_wide, back_land[...].astype(F32).reshape(-1, chain))
    for i in range(owned):
        rows = slice(i * chain, (i + 1) * chain)
        mixed = normalized(strided(back_wide, i, pair_chan, owned), 0)
        tri_update = product(mixed, tri_out_weight[...], 0, 0)
        pair_out[i] = (pair_one[rows] + gate_out[rows] * tri_update).astype(BF16)

    for phase, landing in enumerate((bias_land, msa_land, right_land, tri_land, back_land)):
        drain(send_sems, phase, landing)


def shards(*operands):
    operands = list(operands)
    count = lax.axis_size("res")
    operands[1] = operands[1].reshape(1, -1)
    seqs, chain, channels = operands[2].shape
    owned, _, pair_chan = operands[3].shape
    heads = operands[5].shape[1]
    width = operands[10].shape[1] // 2
    total = seqs * count
    held = pair_chan // count
    vmem = pltpu.VMEM
    group = seqs * owned * channels // LANES
    factor_rows = width * total // LANES * owned
    msa, pair = pl.pallas_call(
        functools.partial(block_kernel, count),
        out_shape=(
            jax.ShapeDtypeStruct((total * owned, channels), BF16),
            jax.ShapeDtypeStruct((owned, chain, pair_chan), BF16),
        ),
        in_specs=[pl.BlockSpec(memory_space=vmem)] * len(operands),
        out_specs=(pl.BlockSpec(memory_space=vmem),) * 2,
        scratch_shapes=[
            vmem((count, owned * heads, chain), BF16),
            vmem((chain // LANES, count * owned * heads, LANES), F32),
            vmem((count, group, LANES), BF16),
            vmem((count, group, LANES), BF16),
            vmem((count, factor_rows, LANES), BF16),
            vmem((width * width, pair_chan), F32),
            vmem((width * total, owned * pair_chan), BF16),
            vmem((chain // LANES, pair_chan * 2 * owned, LANES), F32),
            vmem((count, held * 2 * owned, chain), BF16),
            vmem((count, held * 2 * owned, chain), BF16),
            vmem((count, held * owned, chain), BF16),
            vmem((count, held * owned, chain), BF16),
            vmem((chain // LANES, pair_chan * owned, LANES), F32),
            pltpu.SemaphoreType.DMA((5,)),
            pltpu.SemaphoreType.DMA((5,)),
        ],
        compiler_params=pltpu.CompilerParams(
            collective_id=0, has_side_effects=True, vmem_limit_bytes=60 << 20
        ),
    )(*operands)
    return msa.reshape(total, owned, channels), pair


def solution(mesh):
    placed = (
        P(("crop", "res"), None),
        P("crop"),
        P(("crop", "res"), None, None),
        P(("crop", "res"), None, None),
    ) + (P(),) * 10
    return jax.shard_map(
        shards,
        mesh=mesh,
        in_specs=placed,
        out_specs=(P("crop", "res", None), P(("crop", "res"), None, None)),
        check_vma=False,
    )
```

```python
import functools

import jax
import jax.numpy as jnp
from jax import lax
from jax.experimental import pallas as pl
from jax.experimental.pallas import tpu as pltpu
from jax.sharding import PartitionSpec as P

EPSILON = 1e-05
MESH = pl.DeviceIdType.MESH
F32 = jnp.float32
BF16 = jnp.bfloat16
LANES = 128
SUBLANES = 8


def normalized(rows, axis=-1):
    average = jnp.mean(rows, axis, keepdims=True)
    centred = rows - average
    spread = jnp.mean(centred * centred, axis, keepdims=True)
    return (centred * lax.rsqrt(spread + EPSILON)).astype(BF16)


def product(lhs, rhs, lhs_axis=1, rhs_axis=0):
    return lax.dot_general(
        lhs, rhs, (((lhs_axis,), (rhs_axis,)), ((), ())), preferred_element_type=F32
    )


def permutation(size, major, minor):
    shift = minor.bit_length() - 1
    out = lax.broadcasted_iota(jnp.int32, (size, size), 0)
    came = lax.broadcasted_iota(jnp.int32, (size, size), 1)
    wanted = (out & (minor - 1)) * major + (out >> shift)
    return jnp.where(wanted == came, 1.0, 0.0).astype(BF16)


def swap_halves(first, second):
    half = SUBLANES // 2
    shape = first.shape
    first = first.reshape(-1, SUBLANES, shape[-1])
    second = second.reshape(-1, SUBLANES, shape[-1])
    upper = lax.broadcasted_iota(jnp.int32, first.shape, 1) < half
    low = jnp.where(upper, first, pltpu.roll(second, half, 1))
    high = jnp.where(upper, pltpu.roll(first, half, 1), second)
    return low.reshape(shape), high.reshape(shape)


def strided(wide, first, rows, stride):
    return jnp.concatenate(
        [wide[t, pl.ds(first, rows, stride=stride), :] for t in range(wide.shape[0])], 1
    )


def spread_tiles(wide, rows):
    for t in range(wide.shape[0]):
        wide[t] = rows[:, t * LANES : (t + 1) * LANES]


def attention(projected, channels, head_size, extra):
    rows = projected.shape[0]
    per_tile = LANES // head_size
    owner = lax.broadcasted_iota(jnp.int32, (rows, LANES), 1) >> (head_size.bit_length() - 1)
    pieces = []
    for tile in range(channels // LANES):
        part = lambda block: projected[:, block * channels + tile * LANES :][:, :LANES]
        query = part(0) * head_size ** (-0.5)
        key = part(1).astype(BF16)
        value = part(2)
        queries = jnp.concatenate(
            [jnp.where(owner == t, query, 0.0).astype(BF16) for t in range(per_tile)], 0
        )
        values = jnp.concatenate(
            [jnp.where(owner == t, value, 0.0).astype(BF16) for t in range(per_tile)], 0
        )
        scores = product(queries, key, 1, 1) + jnp.concatenate(
            [extra(tile * per_tile + t) for t in range(per_tile)], 0
        )
        top = jnp.max(scores, -1, keepdims=True)
        raised = jnp.exp(scores - top)
        weights = (raised * (1.0 / jnp.sum(raised, -1, keepdims=True))).astype(BF16)
        weights = jnp.concatenate(
            [weights[t * rows : (t + 1) * rows] for t in range(per_tile)], 1
        )
        mixed = product(weights, values)
        pieces.append((jax.nn.sigmoid(part(3)) * mixed).astype(BF16))
    return jnp.concatenate(pieces, 1)


def block_kernel(
    count,
    ids,
    mask,
    state,
    pair,
    lookup,
    bias_weight,
    row_weight,
    row_readout,
    column_weight,
    column_readout,
    factor_weight,
    outer_weight,
    tri_weight,
    tri_out_weight,
    msa_out,
    pair_out,
    bias_land,
    bias_wide,
    msa_send,
    msa_land,
    right_land,
    outer_wide,
    folded,
    tri_wide,
    tri_send,
    tri_land,
    back_send,
    back_land,
    back_wide,
    send_sems,
    recv_sems,
):
    me = lax.axis_index("res")
    seqs, chain, channels = state.shape
    owned, _, pair_chan = pair.shape
    heads = bias_weight.shape[0]
    head_size = channels // heads
    total = seqs * count
    classes = lookup.shape[0]
    width = factor_weight.shape[0] // 2
    held = pair_chan // count

    barrier = pltpu.get_barrier_semaphore()

    @pl.loop(1, count)
    def _(step):
        pl.semaphore_signal(
            barrier,
            inc=1,
            device_id={"res": me ^ (count - step)},
            device_id_type=MESH,
        )

    def send(phase, landing, outgoing=None):
        @pl.loop(1, count)
        def _(step):
            peer = me ^ (count - step)
            pltpu.make_async_remote_copy(
                src_ref=landing.at[me] if outgoing is None else outgoing.at[peer],
                dst_ref=landing.at[me],
                send_sem=send_sems.at[phase],
                recv_sem=recv_sems.at[phase],
                device_id={"res": peer},
                device_id_type=MESH,
            ).start()

    def drain(sems, phase, landing):
        others = landing.at[pl.ds(0, count - 1)]
        pltpu.make_async_copy(others, others, sems.at[phase]).wait()

    pair_rows = pair[...].astype(F32).reshape(owned * chain, pair_chan)
    bias = product(bias_weight[...], normalized(pair_rows), 1, 1)
    bias_land[me] = jnp.concatenate(
        [bias[:, i * chain : (i + 1) * chain] for i in range(owned)], 0
    ).astype(BF16)
    pl.semaphore_wait(barrier, count - 1)
    send(0, bias_land)

    starts = []
    for s in range(seqs):
        symbols = lax.broadcasted_iota(jnp.int32, (classes, chain), 0)
        hot = jnp.where(symbols == ids[s : s + 1, :], 1.0, 0.0).astype(BF16)
        starts.append(state[s].astype(F32) + product(hot, lookup[...], 0, 0))
    start = jnp.concatenate(starts, 0)
    projected = product(normalized(start), row_weight[...])
    masked = (mask[...].astype(F32) - 1.0) * 10000.0
    drain(recv_sems, 0, bias_land)
    spread_tiles(bias_wide, bias_land[...].astype(F32).reshape(-1, chain) + masked)
    extra = lambda head: strided(bias_wide, head, chain, heads)
    gated = jnp.concatenate(
        [
            attention(projected[s * chain : (s + 1) * chain], channels, head_size, extra)
            for s in range(seqs)
        ],
        0,
    )
    after_rows = (start + product(gated, row_readout[...])).astype(BF16)

    size = seqs * chain
    out = lax.broadcasted_iota(jnp.int32, (size, size), 0)
    came = lax.broadcasted_iota(jnp.int32, (size, size), 1)
    low_bits, seq_bits = owned.bit_length() - 1, seqs.bit_length() - 1
    wanted = (
        ((out >> low_bits) & (seqs - 1)) * chain
        + (out >> (low_bits + seq_bits)) * owned
        + (out & (owned - 1))
    )
    order = jnp.where(wanted == came, 1.0, 0.0).astype(BF16)
    moved = product(order, after_rows)
    group = seqs * owned
    msa_send[...] = jnp.concatenate(
        [
            moved[:, t * LANES : (t + 1) * LANES].reshape(count, group, LANES)
            for t in range(channels // LANES)
        ],
        1,
    ).astype(BF16)
    msa_land[me] = msa_send[me]
    send(1, msa_land, msa_send)
    outer_wide[...] = outer_weight[...].astype(F32)
    by_residue = permutation(total * owned, owned, total)
    by_sequence = permutation(total * owned, total, owned)
    drain(recv_sems, 1, msa_land)

    arrived = msa_land[...].astype(F32)
    arrived = jnp.concatenate(
        [
            arrived[:, t * group : (t + 1) * group].reshape(total * owned, LANES)
            for t in range(channels // LANES)
        ],
        1,
    ).astype(BF16)
    columns = product(by_residue, arrived)
    projected = product(normalized(columns), column_weight[...])
    joined = max(total, LANES)
    bits = total.bit_length() - 1
    same = (lax.broadcasted_iota(jnp.int32, (joined, joined), 0) >> bits) == (
        lax.broadcasted_iota(jnp.int32, (joined, joined), 1) >> bits
    )
    apart = jnp.where(same, 0.0, -1e30)
    gated = jnp.concatenate(
        [
            attention(projected[g : g + joined], channels, head_size, lambda head: apart)
            for g in range(0, total * owned, joined)
        ],
        0,
    )
    after = columns + product(gated, column_readout[...])

    outer_in = normalized(after)
    left = product(outer_in, factor_weight[:width, :], 1, 1).astype(BF16)
    right = product(factor_weight[width:, :], outer_in, 1, 1)
    packed = LANES // total
    slots = width // packed
    right = jnp.concatenate(
        [
            jnp.concatenate(
                [
                    right[p * slots : (p + 1) * slots, r * total : (r + 1) * total]
                    for p in range(packed)
                ],
                1,
            )
            for r in range(owned)
        ],
        0,
    ).astype(BF16)
    right_land[me] = product(permutation(slots * owned, slots, owned), right).astype(BF16)
    send(2, right_land)
    msa_out[...] = (
        product(by_sequence, after.astype(BF16)).reshape(msa_out.shape).astype(BF16)
    )
    for k in range(width):
        slot, p = k // packed, k % packed
        weight = outer_wide[pl.ds(p * slots + slot, width, stride=width), :].astype(BF16)
        part = product(left, weight).astype(BF16)
        for i in range(owned):
            folded[k * total : (k + 1) * total, i * pair_chan : (i + 1) * pair_chan] = part[
                i * total : (i + 1) * total
            ]
    drain(recv_sems, 2, right_land)
    wide = right_land[...].astype(F32)
    tiles = slots * owned // SUBLANES
    wide = wide.reshape(count // 2, 2, tiles, SUBLANES, LANES)
    low, high = swap_halves(wide[:, 0], wide[:, 1])
    right_rows = jnp.concatenate(
        [
            half[:, t].reshape(chain, LANES).astype(BF16)
            for t in range(tiles)
            for half in (low, high)
        ],
        1,
    )
    update = product(right_rows, folded[...]) * (1.0 / total)
    pair_one = pair_rows + jnp.concatenate(
        [update[:, i * pair_chan : (i + 1) * pair_chan] for i in range(owned)], 0
    )

    tri_in = normalized(pair_one)
    factors = product(tri_weight[:, : 4 * pair_chan], tri_in, 0, 1)
    for side in range(2):
        plain = factors[2 * side * pair_chan : (2 * side + 1) * pair_chan]
        gate = factors[(2 * side + 1) * pair_chan : (2 * side + 2) * pair_chan]
        factor = jax.nn.sigmoid(gate) * plain
        for i in range(owned):
            for t in range(chain // LANES):
                tri_wide[t, pl.ds(side * owned + i, pair_chan, stride=2 * owned), :] = factor[
                    :, i * chain + t * LANES :
                ][:, :LANES]
    tri_send[...] = (
        jnp.concatenate([tri_wide[t] for t in range(chain // LANES)], 1)
        .astype(BF16)
        .reshape(tri_send.shape)
    )
    tri_land[me] = tri_send[me]
    send(3, tri_land, tri_send)
    gate_out = jax.nn.sigmoid(product(tri_in, tri_weight[:, 4 * pair_chan :]))
    drain(recv_sems, 3, tri_land)
    wide = tri_land[...].astype(F32).reshape(count // 2, 2, held, SUBLANES, chain)
    low, high = swap_halves(wide[:, 0], wide[:, 1])
    combined = [
        product(
            low[:, c].reshape(chain, chain).astype(BF16),
            high[:, c].reshape(chain, chain).astype(BF16),
            1,
            1,
        ).reshape(count // 2, SUBLANES, chain)
        for c in range(held)
    ]
    swapped = [swap_halves(combined[c], combined[c + 1]) for c in range(0, held, 2)]
    even = jnp.concatenate([low for low, _ in swapped], 1)
    odd = jnp.concatenate([high for _, high in swapped], 1)
    back_send[...] = (
        jnp.concatenate([even[:, None], odd[:, None]], 1)
        .reshape(back_send.shape)
        .astype(BF16)
    )
    back_land[me] = back_send[me]
    send(4, back_land, back_send)
    drain(recv_sems, 4, back_land)
    spread_tiles(back_wide, back_land[...].astype(F32).reshape(-1, chain))
    for i in range(owned):
        rows = slice(i * chain, (i + 1) * chain)
        mixed = normalized(strided(back_wide, i, pair_chan, owned), 0)
        tri_update = product(mixed, tri_out_weight[...], 0, 0)
        pair_out[i] = (pair_one[rows] + gate_out[rows] * tri_update).astype(BF16)

    for phase, landing in enumerate((bias_land, msa_land, right_land, tri_land, back_land)):
        drain(send_sems, phase, landing)


def shards(*operands):
    operands = list(operands)
    count = lax.axis_size("res")
    operands[1] = operands[1].reshape(1, -1)
    operands[5] = operands[5].T
    operands[10] = operands[10].T
    seqs, chain, channels = operands[2].shape
    owned, _, pair_chan = operands[3].shape
    heads = operands[5].shape[0]
    width = operands[10].shape[0] // 2
    total = seqs * count
    held = pair_chan // count
    vmem = pltpu.VMEM
    group = seqs * owned * channels // LANES
    factor_rows = width * total // LANES * owned
    msa, pair = pl.pallas_call(
        functools.partial(block_kernel, count),
        out_shape=(
            jax.ShapeDtypeStruct((total, owned, channels), BF16),
            jax.ShapeDtypeStruct((owned, chain, pair_chan), BF16),
        ),
        in_specs=[pl.BlockSpec(memory_space=vmem)] * len(operands),
        out_specs=(pl.BlockSpec(memory_space=vmem),) * 2,
        scratch_shapes=[
            vmem((count, owned * heads, chain), BF16),
            vmem((chain // LANES, count * owned * heads, LANES), F32),
            vmem((count, group, LANES), BF16),
            vmem((count, group, LANES), BF16),
            vmem((count, factor_rows, LANES), BF16),
            vmem((width * width, pair_chan), F32),
            vmem((width * total, owned * pair_chan), BF16),
            vmem((chain // LANES, pair_chan * 2 * owned, LANES), F32),
            vmem((count, held * 2 * owned, chain), BF16),
            vmem((count, held * 2 * owned, chain), BF16),
            vmem((count, held * owned, chain), BF16),
            vmem((count, held * owned, chain), BF16),
            vmem((chain // LANES, pair_chan * owned, LANES), F32),
            pltpu.SemaphoreType.DMA((5,)),
            pltpu.SemaphoreType.DMA((5,)),
        ],
        compiler_params=pltpu.CompilerParams(
            collective_id=0, has_side_effects=True, vmem_limit_bytes=60 << 20
        ),
    )(*operands)
    return msa, pair


def solution(mesh):
    placed = (
        P(("crop", "res"), None),
        P("crop"),
        P(("crop", "res"), None, None),
        P(("crop", "res"), None, None),
    ) + (P(),) * 10
    return jax.shard_map(
        shards,
        mesh=mesh,
        in_specs=placed,
        out_specs=(P("crop", "res", None), P(("crop", "res"), None, None)),
        check_vma=False,
    )
```
